32 devices in a mesh: row: 2 (over y), col: 16 (over z, x, core).
Axes of the slice: x: 2, y: 2, z: 4, core: 2. Of those that a mesh axis runs over, the one named last changes fastest.
Arguments:
- g_greater: bfloat16 [32, 32, 2, 4096], P('row', 'col'), may hold values from -6 to 6
- g_lesser: bfloat16 [32, 32, 2, 4096], P('row', 'col'), may hold values from -6 to 6
- coupling: float32 [64, 64], replicated, may hold values from 0.5 to 1.5
- partner: int32 [64], replicated, may hold values from 0 to 63, each once
- memory_start: int32 [32], P('row'), may hold values from 0 to 31, as said below
Outputs:
- collision: bfloat16 [32, 4, 2, 4096], P(('row', 'col'))
The draws below stay inside these ranges and needn't reach their ends.
Inputs may be any that keep to these rules, and one draw needn't show every extreme that they name: partner names every orbital once. memory_start[t] lies between 0 and t.
All inputs are finite; a program needn't handle non-finite values.
Results may differ from the reference program's by a relative error of at most 0.0049.
Values may be sent and summed in bfloat16 or wider, within the bound.
A program may use at most 192 MiB of HBM per device.

```python
import math
import jax
import jax.numpy as jnp
from jax import lax

ORB = 64
TW = 4
SPAN = 16
TC = 2
NT = 32
CYCLE = 16
N_ROW = 2


def draw_memory_start(key, part):
    time_ids = jnp.arange(NT, dtype=jnp.int32)
    drawn = jax.random.randint(key, (NT,), 0, time_ids + 1).astype(jnp.int32)
    return jnp.where(time_ids == NT - 1, time_ids, drawn).astype(jnp.int32)


def shard_levels(key, extent, split, smallest, high):
    def one(dim, blocks):
        draws = jax.random.uniform(jax.random.fold_in(jax.random.fold_in(key, 6), dim), (blocks,), jnp.float32, smallest / len(split), high / len(split))
        return jnp.repeat(jnp.exp(draws), extent[dim] // blocks).reshape((-1,) + (1,) * (len(extent) - dim - 1))

    gain = one(*split[0])
    for cut in split[1:]:
        gain = gain * one(*cut)
    return gain


def noise(stream_key, shape, deviation, reach, shards=(), kind=jnp.bfloat16):
    values = deviation * jax.random.normal(stream_key, shape, jnp.float32)
    if shards:
        values = values * shard_levels(stream_key, shape, shards, -0.22, 0.18)
    return jnp.clip(values, -reach, reach).astype(kind)


def setup_inputs(seed: int = 0) -> dict:
    keys = jax.random.split(jax.random.key(seed), 6)
    g_greater = noise(keys[0], (NT, NT, 2, ORB * ORB), 1.0, 6.0, ((0, 2), (1, 16)))
    g_lesser = noise(keys[1], (NT, NT, 2, ORB * ORB), 1.0, 6.0, ((0, 2), (1, 16)))
    coupling = jnp.clip(jax.random.uniform(keys[2], (ORB, ORB), jnp.float32, 0.5, 1.5), 0.5, 1.5)
    partner = jax.random.permutation(keys[3], ORB).astype(jnp.int32)
    memory_start = draw_memory_start(jax.random.fold_in(keys[5], 71), 0)
    return {"g_greater": g_greater, "g_lesser": g_lesser, "coupling": coupling, "partner": partner, "memory_start": memory_start}


def complex_product(left_real, left_imag, right_real, right_imag):
    return (left_real * right_real - left_imag * right_imag, left_real * right_imag + left_imag * right_real)

def self_energy(direct, partnered, mirrored, weight):
    first_pair = complex_product(direct[0], direct[1], partnered[0], partnered[1])
    triple = complex_product(first_pair[0], first_pair[1], mirrored[0], mirrored[1])
    return (weight * triple[0], weight * triple[1])

def split_parts(array):
    return (array[:, 0].astype(jnp.float32), array[:, 1].astype(jnp.float32))

def reference(g_greater, g_lesser, coupling, partner, memory_start):
    pair_count = ORB * ORB
    orbit_ids = jnp.arange(ORB, dtype=jnp.int32)
    permuted = (partner[:, None] * ORB + partner[None, :]).reshape(pair_count).astype(jnp.int32)
    flipped = (orbit_ids[None, :] * ORB + orbit_ids[:, None]).reshape(pair_count).astype(jnp.int32)
    weight = coupling.reshape(pair_count).astype(jnp.float32)
    time_ids = jnp.arange(NT, dtype=jnp.int32)
    stored = (time_ids % CYCLE * TC + time_ids // CYCLE).astype(jnp.int32)
    scaling = 1.0 / (4.0 * math.sqrt(ORB * NT))

    def one_block(block):
        offsets = (block * SPAN + jnp.arange(TW, dtype=jnp.int32)).astype(jnp.int32)
        lesser_slab = jnp.take(g_lesser, stored[offsets], axis=1)
        lesser_slab = lesser_slab.reshape(NT, TW, 2, ORB, ORB).astype(jnp.float32)
        slab_real = lesser_slab[:, :, 0]
        slab_imag = lesser_slab[:, :, 1]

        def one_time(moment):
            row_greater = jnp.take(lax.dynamic_index_in_dim(g_greater, moment, 0, False), stored, axis=0)
            row_lesser = jnp.take(lax.dynamic_index_in_dim(g_lesser, moment, 0, False), stored, axis=0)
            stored_col = stored[moment]
            back_greater = lax.dynamic_index_in_dim(g_greater, stored_col, 1, False)
            back_lesser = lax.dynamic_index_in_dim(g_lesser, stored_col, 1, False)
            greater_sig = self_energy(split_parts(row_greater), split_parts(jnp.take(row_greater, permuted, axis=2)), split_parts(jnp.take(back_lesser, flipped, axis=2)), weight)
            lesser_sig = self_energy(split_parts(row_lesser), split_parts(jnp.take(row_lesser, permuted, axis=2)), split_parts(jnp.take(back_greater, flipped, axis=2)), weight)
            live_mask = ((time_ids >= memory_start[moment]) & (time_ids <= moment))[:, None]
            ret_real = jnp.where(live_mask, greater_sig[0] - lesser_sig[0], 0.0)
            ret_imag = jnp.where(live_mask, greater_sig[1] - lesser_sig[1], 0.0)
            ret_real = lax.optimization_barrier(ret_real.astype(jnp.bfloat16)).astype(jnp.float32).reshape(NT, ORB, ORB)
            ret_imag = lax.optimization_barrier(ret_imag.astype(jnp.bfloat16)).astype(jnp.float32).reshape(NT, ORB, ORB)
            out_real = jnp.einsum('sik,swkl->wil', ret_real, slab_real) - jnp.einsum('sik,swkl->wil', ret_imag, slab_imag)
            out_imag = jnp.einsum('sik,swkl->wil', ret_real, slab_imag) + jnp.einsum('sik,swkl->wil', ret_imag, slab_real)
            joined = jnp.stack([out_real, out_imag], axis=1) * scaling
            return joined.reshape(TW, 2, pair_count).astype(jnp.bfloat16)
        return lax.map(one_time, (block * SPAN + jnp.arange(SPAN, dtype=jnp.int32)).astype(jnp.int32))
    result = lax.map(one_block, jnp.arange(N_ROW, dtype=jnp.int32))
    return result.reshape(NT, TW, 2, pair_count)
```

```python
import functools
import math

import jax
import jax.numpy as jnp
from jax import lax
from jax.experimental import pallas as pl
from jax.experimental.pallas import tpu as pltpu
from jax.sharding import PartitionSpec as P

TW = 4
MESH = pl.DeviceIdType.MESH


def kernel(
    rows,
    cols,
    scaling,
    memory_ref,
    greater_ref,
    lesser_ref,
    swap_ref,
    swap_t_ref,
    weight_ref,
    out_ref,
    direct_greater,
    direct_lesser,
    mirror_greater,
    mirror_lesser,
    slab,
    total,
    direct_send,
    direct_recv,
    mirror_send,
    mirror_recv,
    slab_send,
    slab_recv,
    own_sem,
):
    row = lax.axis_index("row")
    col = lax.axis_index("col")
    orbits = greater_ref.shape[2]
    groups = cols // TW
    group = col // TW
    place = col % TW
    sources = (greater_ref, lesser_ref)
    directs = (direct_greater, direct_lesser)
    mirrors = (mirror_greater, mirror_lesser)

    barrier = pltpu.get_barrier_semaphore()

    def greet_col(step, carry):
        pl.semaphore_signal(
            barrier, inc=1, device_id=(row, lax.rem(col + step, cols)), device_id_type=MESH
        )
        return carry

    def greet_row(step, carry):
        pl.semaphore_signal(
            barrier, inc=1, device_id=(lax.rem(row + step, rows), col), device_id_type=MESH
        )
        return carry

    lax.fori_loop(1, cols, greet_col, 0)
    lax.fori_loop(1, rows, greet_row, 0)

    def own_copies():
        copies = []
        for f in range(2):
            copies.append(
                pltpu.make_async_copy(sources[f].at[col], directs[f].at[col], own_sem.at[f])
            )
            copies.append(
                pltpu.make_async_copy(
                    sources[f].at[:, row], mirrors[f].at[row], own_sem.at[2 + f]
                )
            )
        return copies

    for copy in own_copies():
        copy.start()
    pl.semaphore_wait(barrier, cols - 1 + rows - 1)

    def mirror_copy(f, other, holder):
        return pltpu.make_async_remote_copy(
            src_ref=sources[f].at[:, other],
            dst_ref=mirrors[f].at[holder],
            send_sem=mirror_send.at[f, other],
            recv_sem=mirror_recv.at[f, holder],
            device_id=(other, col),
            device_id_type=MESH,
        )

    for other in range(1, rows):
        @pl.when(other > row)
        def _(other=other):
            for f in (1, 0):
                mirror_copy(f, other, row).start()

    def direct_copy(f, target, holder):
        return pltpu.make_async_remote_copy(
            src_ref=sources[f].at[target],
            dst_ref=directs[f].at[holder],
            send_sem=direct_send.at[f, target],
            recv_sem=direct_recv.at[f, holder],
            device_id=(row, target),
            device_id_type=MESH,
        )

    def send_direct(step, carry):
        target = lax.rem(col + step, cols)
        for f in range(2):
            direct_copy(f, target, col).start()
        return carry

    lax.fori_loop(1, cols, send_direct, 0)

    def slab_copy(kind, w, k, target):
        return pltpu.make_async_remote_copy(
            src_ref=slab.at[w, k],
            dst_ref=slab.at[w, k],
            send_sem=slab_send.at[kind, k],
            recv_sem=slab_recv.at[w, k],
            device_id=(row, target),
            device_id_type=MESH,
        )

    base = group * TW
    near = base + place + 1 - 2 * lax.rem(place, 2)
    across_place = lax.rem(place + 2, TW)
    across = base + across_place
    corner_place = across_place + 1 - 2 * lax.rem(across_place, 2)
    near_place = place + 1 - 2 * lax.rem(place, 2)
    following = lax.rem(col + TW, cols)

    for copy in own_copies():
        copy.wait()

    for k in range(rows):
        @pl.when(k <= row)
        def _(k=k):
            @pl.when(k < row)
            def _():
                for f in range(2):
                    mirror_copy(f, row, k).wait_recv()

            @pl.when(group == 0)
            def _():
                copy = pltpu.make_async_copy(
                    mirror_lesser.at[k], slab.at[place, k], own_sem.at[4]
                )
                copy.start()
                copy.wait()

            @pl.when(group > 0)
            def _():
                slab_copy(0, place, k, following).wait_recv()

            @pl.when(group < groups - 1)
            def _():
                slab_copy(0, place, k, following).start()

            slab_copy(1, place, k, across).start()
            slab_copy(2, place, k, near).start()

    for k in range(rows):
        @pl.when(k <= row)
        def _(k=k):
            slab_copy(1, across_place, k, across).wait_recv()
            slab_copy(3, across_place, k, near).start()

    def wait_direct(step, carry):
        holder = lax.rem(col + step, cols)
        for f in range(2):
            direct_copy(f, holder, holder).wait_recv()
        return carry

    lax.fori_loop(1, cols, wait_direct, 0)

    for k in range(rows):
        @pl.when(k <= row)
        def _(k=k):
            slab_copy(2, near_place, k, near).wait_recv()
            slab_copy(3, corner_place, k, near).wait_recv()

    total[...] = jnp.zeros_like(total)
    swap = swap_ref[...]
    swap_t = swap_t_ref[...]
    weight = weight_ref[...]
    moment = row * cols + col
    earliest = memory_ref[col]
    lane = lax.broadcasted_iota(jnp.int32, (orbits, 2 * orbits), 1)
    half = (lane >= orbits).astype(jnp.int32)
    wide = 2 * orbits

    def energy(direct, mirrored):
        tile = direct.reshape(wide, wide)
        turned = jnp.concatenate(
            [
                jnp.concatenate([tile[:orbits, :orbits], tile[orbits:, :orbits]], axis=1),
                jnp.concatenate([tile[:orbits, orbits:], tile[orbits:, orbits:]], axis=1),
            ],
            axis=0,
        )
        swapped = jnp.dot(swap, turned, preferred_element_type=jnp.float32).astype(jnp.bfloat16)
        swapped = jnp.dot(swapped, swap_t, preferred_element_type=jnp.float32)
        back = mirrored.reshape(wide, wide).astype(jnp.float32).T
        turned = turned.astype(jnp.float32)
        ar, ai = turned[:orbits], turned[orbits:]
        br, bi = swapped[:orbits], swapped[orbits:]
        mr, mi = back[:orbits], back[orbits:]
        fr = ar * br - ai * bi
        fi = ar * bi + ai * br
        return (weight * (fr * mr - fi * mi), weight * (fr * mi + fi * mr))

    for k in range(rows):
        @pl.when(k <= row)
        def _(k=k):
            def one_pair(pair, carry):
                at = pl.ds(2 * pair, 2)
                up = energy(direct_greater[at, k], mirror_lesser[k, at])
                down = energy(direct_lesser[at, k], mirror_greater[k, at])
                second = k * cols + 2 * pair + half
                live = (second >= earliest) & (second <= moment)
                retarded = jnp.concatenate(
                    [
                        jnp.where(live, up[0] - down[0], 0.0),
                        jnp.where(live, up[1] - down[1], 0.0),
                    ],
                    axis=0,
                ).astype(jnp.bfloat16)
                for w in range(TW):
                    total[w] += jnp.dot(
                        retarded,
                        slab[w, k, at].reshape(wide, wide),
                        preferred_element_type=jnp.float32,
                    )
                return carry

            lax.fori_loop(0, cols // 2, one_pair, 0)

    for w in range(TW):
        whole = total[w]
        out_ref[w, 0] = (
            (whole[:orbits, :orbits] - whole[orbits:, orbits:]) * scaling
        ).astype(jnp.bfloat16)
        out_ref[w, 1] = (
            (whole[:orbits, orbits:] + whole[orbits:, :orbits]) * scaling
        ).astype(jnp.bfloat16)

    def drain_direct(step, carry):
        target = lax.rem(col + step, cols)
        for f in range(2):
            direct_copy(f, target, col).wait_send()
        return carry

    lax.fori_loop(1, cols, drain_direct, 0)
    for k in range(rows):
        @pl.when(k <= row)
        def _(k=k):
            @pl.when(group < groups - 1)
            def _():
                slab_copy(0, place, k, following).wait_send()

            slab_copy(1, place, k, across).wait_send()
            slab_copy(2, place, k, near).wait_send()
            slab_copy(3, across_place, k, near).wait_send()

    for other in range(1, rows):
        @pl.when(other > row)
        def _(other=other):
            for f in range(2):
                mirror_copy(f, other, row).wait_send()


def matrices(tiles, orbits):
    first, second, components, _ = tiles.shape
    return (
        tiles.reshape(first, second, components, orbits, orbits)
        .transpose(0, 1, 3, 2, 4)
        .reshape(first, second, orbits, components * orbits)
    )


def per_device(g_greater, g_lesser, coupling, partner, memory_start):
    tile_rows, tile_cols, components, pair_count = g_greater.shape
    rows = lax.axis_size("row")
    cols = lax.axis_size("col")
    orbits = coupling.shape[0]
    wide = 2 * orbits
    scaling = 1.0 / (4.0 * math.sqrt(orbits * tile_rows * rows))
    ids = jnp.arange(wide, dtype=jnp.int32)
    both = jnp.concatenate([partner, partner + orbits])
    swap = (both[:, None] == ids[None, :]).astype(jnp.bfloat16)
    swap_t = (ids[:, None] == both[None, :]).astype(jnp.bfloat16)
    weight = jnp.concatenate([coupling, coupling], axis=1)
    tile = (orbits, wide)
    vmem = pl.BlockSpec(memory_space=pltpu.VMEM)
    out = pl.pallas_call(
        functools.partial(kernel, rows, cols, scaling),
        out_shape=jax.ShapeDtypeStruct((TW, 2, orbits, orbits), jnp.bfloat16),
        in_specs=[
            pl.BlockSpec(memory_space=pltpu.SMEM),
            pl.BlockSpec(memory_space=pl.ANY),
            pl.BlockSpec(memory_space=pl.ANY),
            vmem,
            vmem,
            vmem,
        ],
        out_specs=vmem,
        scratch_shapes=[
            pltpu.VMEM((cols, rows) + tile, jnp.bfloat16),
            pltpu.VMEM((cols, rows) + tile, jnp.bfloat16),
            pltpu.VMEM((rows, cols) + tile, jnp.bfloat16),
            pltpu.VMEM((rows, cols) + tile, jnp.bfloat16),
            pltpu.VMEM((TW, rows, cols) + tile, jnp.bfloat16),
            pltpu.VMEM((TW, wide, wide), jnp.float32),
            pltpu.SemaphoreType.DMA((2, cols)),
            pltpu.SemaphoreType.DMA((2, cols)),
            pltpu.SemaphoreType.DMA((2, rows)),
            pltpu.SemaphoreType.DMA((2, rows)),
            pltpu.SemaphoreType.DMA((4, rows)),
            pltpu.SemaphoreType.DMA((TW, rows)),
            pltpu.SemaphoreType.DMA((5,)),
        ],
        compiler_params=pltpu.CompilerParams(
            collective_id=0, has_side_effects=True, vmem_limit_bytes=48 * 1024 * 1024
        ),
    )(
        memory_start,
        matrices(g_greater, orbits),
        matrices(g_lesser, orbits),
        swap,
        swap_t,
        weight,
    )
    return out.reshape(1, TW, 2, pair_count)


def solution(mesh):
    return jax.shard_map(
        per_device,
        mesh=mesh,
        in_specs=(P("row", "col", None, None), P("row", "col", None, None), P(), P(), P("row")),
        out_specs=P(("row", "col"), None, None, None),
        check_vma=False,
    )
```

```python
import functools
import math

import jax
import jax.numpy as jnp
from jax import lax
from jax.experimental import pallas as pl
from jax.experimental.pallas import tpu as pltpu
from jax.sharding import PartitionSpec as P

TW = 4
CHUNKS = 4
MESH = pl.DeviceIdType.MESH


def kernel(
    rows,
    cols,
    scaling,
    memory_ref,
    greater_ref,
    lesser_ref,
    partner_ref,
    coupling_ref,
    out_ref,
    direct_greater,
    direct_lesser,
    mirror_greater,
    mirror_lesser,
    slab,
    transit,
    kept,
    total,
    direct_send,
    direct_recv,
    mirror_send,
    mirror_recv,
    slab_send,
    slab_recv,
    transit_send,
    transit_recv,
    own_sem,
):
    row = lax.axis_index("row")
    col = lax.axis_index("col")
    orbits = greater_ref.shape[2]
    wide = 2 * orbits
    groups = cols // TW
    group = col // TW
    place = lax.rem(col, TW)
    base = group * TW
    chunk = cols // CHUNKS
    sources = (greater_ref, lesser_ref)
    directs = (direct_greater, direct_lesser)
    mirrors = (mirror_greater, mirror_lesser)

    barrier = pltpu.get_barrier_semaphore()

    def greet_col(step, carry):
        pl.semaphore_signal(
            barrier, inc=1, device_id=(row, lax.rem(col + step, cols)), device_id_type=MESH
        )
        return carry

    def greet_row(step, carry):
        pl.semaphore_signal(
            barrier, inc=1, device_id=(lax.rem(row + step, rows), col), device_id_type=MESH
        )
        return carry

    lax.fori_loop(1, cols, greet_col, 0)
    lax.fori_loop(1, rows, greet_row, 0)

    def own_copies():
        copies = []
        for f in range(2):
            copies.append(
                pltpu.make_async_copy(sources[f].at[col], directs[f].at[col], own_sem.at[f])
            )
            copies.append(
                pltpu.make_async_copy(
                    sources[f].at[:, row], mirrors[f].at[row], own_sem.at[2 + f]
                )
            )
        return copies

    def own_slab():
        return pltpu.make_async_copy(
            lesser_ref.at[:, row], slab.at[place, row], own_sem.at[4]
        )

    for copy in own_copies():
        copy.start()

    def own_transit(other):
        return pltpu.make_async_copy(
            lesser_ref.at[:, other], transit.at[other], own_sem.at[4 + other]
        )

    @pl.when(group == 0)
    def _():
        own_slab().start()
        for other in range(1, rows):
            @pl.when(other > row)
            def _(other=other):
                own_transit(other).start()

    partners = partner_ref[...]
    partners = jnp.concatenate([partners, partners + orbits], axis=1)
    places = lax.broadcasted_iota(jnp.int32, (wide, wide), 0)
    swap_wide = jnp.where(places == partners, 1.0, 0.0)
    swap_t = swap_wide.astype(jnp.bfloat16)
    swap = swap_wide.T.astype(jnp.bfloat16)
    weight = jnp.concatenate([coupling_ref[...], coupling_ref[...]], axis=1)
    total[...] = jnp.zeros_like(total)

    pl.semaphore_wait(barrier, cols - 1 + rows - 1)

    def mirror_copy(f, other, holder):
        return pltpu.make_async_remote_copy(
            src_ref=sources[f].at[:, other],
            dst_ref=mirrors[f].at[holder],
            send_sem=mirror_send.at[f, other],
            recv_sem=mirror_recv.at[f, holder],
            device_id=(other, col),
            device_id_type=MESH,
        )

    for f in (1, 0):
        for other in range(1, rows):
            @pl.when(other > row)
            def _(other=other, f=f):
                mirror_copy(f, other, row).start()

    def direct_copy(f, target, holder, k):
        return pltpu.make_async_remote_copy(
            src_ref=sources[f].at[target, k],
            dst_ref=directs[f].at[holder, k],
            send_sem=direct_send.at[f, target, k],
            recv_sem=direct_recv.at[f, holder, k],
            device_id=(row, target),
            device_id_type=MESH,
        )

    def send_edge(target, act):
        @pl.when(target != col)
        def _():
            for f in range(2):
                act(direct_copy(f, target, col, row))

    def send_body(target, act):
        @pl.when(target != col)
        def _():
            for k in range(rows - 1):
                @pl.when(k < row)
                def _(k=k):
                    for f in range(2):
                        act(direct_copy(f, target, col, k))

    def start_edge(target, carry):
        send_edge(target, lambda copy: copy.start())
        return carry

    def start_body(target, carry):
        send_body(target, lambda copy: copy.start())
        return carry

    def slab_copy(kind, w, k, h, target):
        return pltpu.make_async_remote_copy(
            src_ref=slab.at[w, k, pl.ds(h * chunk, chunk)],
            dst_ref=slab.at[w, k, pl.ds(h * chunk, chunk)],
            send_sem=slab_send.at[kind, k, h],
            recv_sem=slab_recv.at[w, k, h],
            device_id=(row, target),
            device_id_type=MESH,
        )

    near_place = place + 1 - 2 * lax.rem(place, 2)
    across_place = lax.rem(place + 2, TW)
    corner_place = across_place + 1 - 2 * lax.rem(across_place, 2)
    near = base + near_place
    across = base + across_place
    following = lax.rem(col + TW, cols)

    def transit_copy(kind, other, h, to):
        piece = pl.ds(h * chunk, chunk)
        if kind == 0:
            return pltpu.make_async_remote_copy(
                src_ref=transit.at[other, piece],
                dst_ref=transit.at[other, piece],
                send_sem=transit_send.at[0, other, h],
                recv_sem=transit_recv.at[other, h],
                device_id=(row, following),
                device_id_type=MESH,
            )
        return pltpu.make_async_remote_copy(
            src_ref=transit.at[other, piece],
            dst_ref=slab.at[place, to, piece],
            send_sem=transit_send.at[1, other, h],
            recv_sem=slab_recv.at[place, to, h],
            device_id=(other, col),
            device_id_type=MESH,
        )

    def spread(k, h):
        slab_copy(1, place, k, h, across).start()
        slab_copy(2, place, k, h, near).start()

    def forward(copy):
        @pl.when(group < groups - 1)
        def _():
            copy.start()

    @pl.when(group == 0)
    def _():
        own_slab().wait()
        for h in range(CHUNKS):
            forward(slab_copy(0, place, row, h, following))
        for other in range(1, rows):
            @pl.when(other > row)
            def _(other=other):
                own_transit(other).wait()
                for h in range(CHUNKS):
                    forward(transit_copy(0, other, h, row))
                    transit_copy(1, other, h, row).start()
        for h in range(CHUNKS):
            spread(row, h)

    lax.fori_loop(col, cols, start_edge, 0)
    late = jnp.where(group == 0, 0, base + TW)
    lax.fori_loop(0, late, start_body, 0)

    @pl.when(group > 0)
    def _():
        for h in range(CHUNKS):
            slab_copy(0, place, row, h, following).wait_recv()
            forward(slab_copy(0, place, row, h, following))
            spread(row, h)
        for other in range(1, rows):
            @pl.when(other > row)
            def _(other=other):
                for h in range(CHUNKS):
                    transit_copy(0, other, h, row).wait_recv()
                    forward(transit_copy(0, other, h, row))
                    transit_copy(1, other, h, row).start()

    lax.fori_loop(late, cols, start_body, 0)

    def spread_again(k):
        for h in range(CHUNKS):
            slab_copy(1, across_place, k, h, across).wait_recv()
            slab_copy(3, across_place, k, h, near).start()

    spread_again(row)

    for copy in own_copies():
        copy.wait()

    moment = row * cols + col
    earliest = memory_ref[col]
    lane = lax.broadcasted_iota(jnp.int32, (orbits, wide), 1)
    half = (lane >= orbits).astype(jnp.int32)
    depth = lax.broadcasted_iota(jnp.int32, (wide, wide), 0)
    depth_half = (depth >= orbits).astype(jnp.int32)

    def energy(direct, mirrored, seen):
        tile = jnp.where(seen, direct.reshape(wide, wide).astype(jnp.float32), 0.0)
        turned = jnp.concatenate(
            [
                jnp.concatenate([tile[:orbits, :orbits], tile[orbits:, :orbits]], axis=1),
                jnp.concatenate([tile[:orbits, orbits:], tile[orbits:, orbits:]], axis=1),
            ],
            axis=0,
        )
        swapped = jnp.dot(
            swap, turned.astype(jnp.bfloat16), preferred_element_type=jnp.float32
        ).astype(jnp.bfloat16)
        swapped = jnp.dot(swapped, swap_t, preferred_element_type=jnp.float32)
        back = mirrored.reshape(wide, wide).astype(jnp.float32).T
        ar, ai = turned[:orbits], turned[orbits:]
        br, bi = swapped[:orbits], swapped[orbits:]
        mr, mi = back[:orbits], back[orbits:]
        fr = ar * br - ai * bi
        fi = ar * bi + ai * br
        return (weight * (fr * mr - fi * mi), weight * (fr * mi + fi * mr))

    def wait_direct(holder, k):
        @pl.when((holder != col) & ((k < row) | (holder <= col)))
        def _():
            for f in range(2):
                direct_copy(f, holder, holder, k).wait_recv()

    for j in range(rows):
        @pl.when(j <= row)
        def _(j=j):
            k = row - j
            if j > 0:
                for h in range(CHUNKS):
                    transit_copy(1, row, h, k).wait_recv()
                    spread(k, h)
                for f in range(2):
                    mirror_copy(f, row, k).wait_recv()
                spread_again(k)

            def one_pair(pair, carry):
                wait_direct(2 * pair, k)
                wait_direct(2 * pair + 1, k)
                at = pl.ds(2 * pair, 2)
                start = k * cols + 2 * pair
                seen = start + depth_half <= moment
                up = energy(direct_greater[at, k], mirror_lesser[k, at], seen)
                down = energy(direct_lesser[at, k], mirror_greater[k, at], seen)
                second = start + half
                live = (second >= earliest) & (second <= moment)
                kept[k, pair] = jnp.concatenate(
                    [
                        jnp.where(live, up[0] - down[0], 0.0),
                        jnp.where(live, up[1] - down[1], 0.0),
                    ],
                    axis=0,
                ).astype(jnp.bfloat16)
                return carry

            lax.fori_loop(0, jnp.where(k < row, cols // 2, col // 2 + 1), one_pair, 0)

    for j in range(rows):
        @pl.when(j <= row)
        def _(j=j):
            k = row - j
            for h in range(CHUNKS):
                slab_copy(2, near_place, k, h, near).wait_recv()
                slab_copy(3, corner_place, k, h, near).wait_recv()

            def one_product(pair, carry):
                at = pl.ds(2 * pair, 2)
                for w in range(TW):
                    total[w] += jnp.dot(
                        kept[k, pair],
                        slab[w, k, at].reshape(wide, wide),
                        preferred_element_type=jnp.float32,
                    )
                return carry

            lax.fori_loop(0, jnp.where(k < row, cols // 2, col // 2 + 1), one_product, 0)

    for w in range(TW):
        whole = total[w]
        out_ref[w, 0] = (
            (whole[:orbits, :orbits] - whole[orbits:, orbits:]) * scaling
        ).astype(jnp.bfloat16)
        out_ref[w, 1] = (
            (whole[:orbits, orbits:] + whole[orbits:, :orbits]) * scaling
        ).astype(jnp.bfloat16)

    def drain_edge(target, carry):
        send_edge(target, lambda copy: copy.wait_send())
        return carry

    def drain_body(target, carry):
        send_body(target, lambda copy: copy.wait_send())
        return carry

    lax.fori_loop(col, cols, drain_edge, 0)
    lax.fori_loop(0, cols, drain_body, 0)
    for h in range(CHUNKS):
        @pl.when(group < groups - 1)
        def _(h=h):
            slab_copy(0, place, row, h, following).wait_send()

    for k in range(rows):
        @pl.when(k <= row)
        def _(k=k):
            for h in range(CHUNKS):
                slab_copy(1, place, k, h, across).wait_send()
                slab_copy(2, place, k, h, near).wait_send()
                slab_copy(3, across_place, k, h, near).wait_send()

    for other in range(1, rows):
        @pl.when(other > row)
        def _(other=other):
            for h in range(CHUNKS):
                @pl.when(group < groups - 1)
                def _(h=h):
                    transit_copy(0, other, h, row).wait_send()

                transit_copy(1, other, h, row).wait_send()

    for other in range(1, rows):
        @pl.when(other > row)
        def _(other=other):
            for f in range(2):
                mirror_copy(f, other, row).wait_send()


def matrices(tiles, orbits):
    first, second, components, _ = tiles.shape
    return (
        tiles.reshape(first, second, components, orbits, orbits)
        .transpose(0, 1, 3, 2, 4)
        .reshape(first, second, orbits, components * orbits)
    )


def per_device(g_greater, g_lesser, coupling, partner, memory_start):
    tile_rows, tile_cols, components, pair_count = g_greater.shape
    rows = lax.axis_size("row")
    cols = lax.axis_size("col")
    orbits = coupling.shape[0]
    wide = 2 * orbits
    scaling = 1.0 / (4.0 * math.sqrt(orbits * tile_rows * rows))
    tile = (orbits, wide)
    vmem = pl.BlockSpec(memory_space=pltpu.VMEM)
    out = pl.pallas_call(
        functools.partial(kernel, rows, cols, scaling),
        out_shape=jax.ShapeDtypeStruct((TW, 2, orbits, orbits), jnp.bfloat16),
        in_specs=[
            pl.BlockSpec(memory_space=pltpu.SMEM),
            pl.BlockSpec(memory_space=pl.ANY),
            pl.BlockSpec(memory_space=pl.ANY),
            vmem,
            vmem,
        ],
        out_specs=vmem,
        scratch_shapes=[
            pltpu.VMEM((cols, rows) + tile, jnp.bfloat16),
            pltpu.VMEM((cols, rows) + tile, jnp.bfloat16),
            pltpu.VMEM((rows, cols) + tile, jnp.bfloat16),
            pltpu.VMEM((rows, cols) + tile, jnp.bfloat16),
            pltpu.VMEM((TW, rows, cols) + tile, jnp.bfloat16),
            pltpu.VMEM((rows, cols) + tile, jnp.bfloat16),
            pltpu.VMEM((rows, cols // 2, wide, wide), jnp.bfloat16),
            pltpu.VMEM((TW, wide, wide), jnp.float32),
            pltpu.SemaphoreType.DMA((2, cols, rows)),
            pltpu.SemaphoreType.DMA((2, cols, rows)),
            pltpu.SemaphoreType.DMA((2, rows)),
            pltpu.SemaphoreType.DMA((2, rows)),
            pltpu.SemaphoreType.DMA((4, rows, CHUNKS)),
            pltpu.SemaphoreType.DMA((TW, rows, CHUNKS)),
            pltpu.SemaphoreType.DMA((2, rows, CHUNKS)),
            pltpu.SemaphoreType.DMA((rows, CHUNKS)),
            pltpu.SemaphoreType.DMA((4 + rows,)),
        ],
        compiler_params=pltpu.CompilerParams(
            collective_id=0, has_side_effects=True, vmem_limit_bytes=48 * 1024 * 1024
        ),
    )(
        memory_start,
        matrices(g_greater, orbits),
        matrices(g_lesser, orbits),
        partner.reshape(1, orbits),
        coupling,
    )
    return out.reshape(1, TW, 2, pair_count)


def solution(mesh):
    return jax.shard_map(
        per_device,
        mesh=mesh,
        in_specs=(P("row", "col", None, None), P("row", "col", None, None), P(), P(), P("row")),
        out_specs=P(("row", "col"), None, None, None),
        check_vma=False,
    )
```

```python
import functools
import math

import jax
import jax.numpy as jnp
from jax import lax
from jax.experimental import pallas as pl
from jax.experimental.pallas import tpu as pltpu
from jax.sharding import PartitionSpec as P

TW = 4
CHUNKS = 8
MESH = pl.DeviceIdType.MESH


def kernel(
    rows,
    cols,
    scaling,
    memory_ref,
    greater_ref,
    lesser_ref,
    partner_ref,
    coupling_ref,
    out_ref,
    direct_greater,
    direct_lesser,
    mirror_greater,
    mirror_lesser,
    slab,
    transit,
    kept,
    total,
    direct_send,
    direct_recv,
    mirror_send,
    mirror_recv,
    slab_send,
    slab_recv,
    transit_send,
    transit_recv,
    own_sem,
):
    row = lax.axis_index("row")
    col = lax.axis_index("col")
    orbits = greater_ref.shape[2]
    wide = 2 * orbits
    groups = cols // TW
    group = col // TW
    place = lax.rem(col, TW)
    base = group * TW
    chunk = cols // CHUNKS
    sources = (greater_ref, lesser_ref)
    directs = (direct_greater, direct_lesser)
    mirrors = (mirror_greater, mirror_lesser)

    barrier = pltpu.get_barrier_semaphore()

    def greet_col(step, carry):
        pl.semaphore_signal(
            barrier, inc=1, device_id=(row, lax.rem(col + step, cols)), device_id_type=MESH
        )
        return carry

    def greet_row(step, carry):
        pl.semaphore_signal(
            barrier, inc=1, device_id=(lax.rem(row + step, rows), col), device_id_type=MESH
        )
        return carry

    lax.fori_loop(1, cols, greet_col, 0)
    lax.fori_loop(1, rows, greet_row, 0)

    def own_copies():
        copies = []
        for f in range(2):
            copies.append(
                pltpu.make_async_copy(sources[f].at[col], directs[f].at[col], own_sem.at[f])
            )
            copies.append(
                pltpu.make_async_copy(
                    sources[f].at[:, row], mirrors[f].at[row], own_sem.at[2 + f]
                )
            )
        return copies

    def own_slab():
        return pltpu.make_async_copy(
            lesser_ref.at[:, row], slab.at[place, row], own_sem.at[4]
        )

    for copy in own_copies():
        copy.start()

    def own_transit(other):
        return pltpu.make_async_copy(
            lesser_ref.at[:, other], transit.at[other], own_sem.at[4 + other]
        )

    @pl.when(group == 0)
    def _():
        own_slab().start()
        for other in range(1, rows):
            @pl.when(other > row)
            def _(other=other):
                own_transit(other).start()

    partners = partner_ref[...]
    partners = jnp.concatenate([partners, partners + orbits], axis=1)
    places = lax.broadcasted_iota(jnp.int32, (wide, wide), 0)
    swap_wide = jnp.where(places == partners, 1.0, 0.0)
    swap_t = swap_wide.astype(jnp.bfloat16)
    swap = swap_wide.T.astype(jnp.bfloat16)
    weight = jnp.concatenate([coupling_ref[...], coupling_ref[...]], axis=1)
    total[...] = jnp.zeros_like(total)

    pl.semaphore_wait(barrier, cols - 1 + rows - 1)

    def mirror_copy(f, other, holder):
        return pltpu.make_async_remote_copy(
            src_ref=sources[f].at[:, other],
            dst_ref=mirrors[f].at[holder],
            send_sem=mirror_send.at[f, other],
            recv_sem=mirror_recv.at[f, holder],
            device_id=(other, col),
            device_id_type=MESH,
        )

    for f in (1, 0):
        for other in range(1, rows):
            @pl.when(other > row)
            def _(other=other, f=f):
                mirror_copy(f, other, row).start()

    def direct_copy(f, target, holder, k):
        return pltpu.make_async_remote_copy(
            src_ref=sources[f].at[target, k],
            dst_ref=directs[f].at[holder, k],
            send_sem=direct_send.at[f, target, k],
            recv_sem=direct_recv.at[f, holder, k],
            device_id=(row, target),
            device_id_type=MESH,
        )

    def send_edge(target, act):
        @pl.when(target != col)
        def _():
            for f in range(2):
                act(direct_copy(f, target, col, row))

    def send_body(target, act):
        @pl.when(target != col)
        def _():
            for k in range(rows - 1):
                @pl.when(k < row)
                def _(k=k):
                    for f in range(2):
                        act(direct_copy(f, target, col, k))

    def start_edge(target, carry):
        send_edge(target, lambda copy: copy.start())
        return carry

    def start_body(target, carry):
        send_body(target, lambda copy: copy.start())
        return carry

    def slab_copy(kind, w, k, h, target):
        return pltpu.make_async_remote_copy(
            src_ref=slab.at[w, k, pl.ds(h * chunk, chunk)],
            dst_ref=slab.at[w, k, pl.ds(h * chunk, chunk)],
            send_sem=slab_send.at[kind, k, h],
            recv_sem=slab_recv.at[w, k, h],
            device_id=(row, target),
            device_id_type=MESH,
        )

    near_place = place + 1 - 2 * lax.rem(place, 2)
    across_place = lax.rem(place + 2, TW)
    corner_place = across_place + 1 - 2 * lax.rem(across_place, 2)
    near = base + near_place
    across = base + across_place
    following = lax.rem(col + TW, cols)

    def transit_copy(kind, other, h, to):
        piece = pl.ds(h * chunk, chunk)
        if kind == 0:
            return pltpu.make_async_remote_copy(
                src_ref=transit.at[other, piece],
                dst_ref=transit.at[other, piece],
                send_sem=transit_send.at[0, other, h],
                recv_sem=transit_recv.at[other, h],
                device_id=(row, following),
                device_id_type=MESH,
            )
        return pltpu.make_async_remote_copy(
            src_ref=transit.at[other, piece],
            dst_ref=slab.at[place, to, piece],
            send_sem=transit_send.at[1, other, h],
            recv_sem=slab_recv.at[place, to, h],
            device_id=(other, col),
            device_id_type=MESH,
        )

    def spread(k, h):
        slab_copy(2, place, k, h, near).start()
        slab_copy(1, place, k, h, across).start()

    def forward(copy):
        @pl.when(group < groups - 1)
        def _():
            copy.start()

    @pl.when(group == 0)
    def _():
        own_slab().wait()
        for h in range(CHUNKS):
            forward(slab_copy(0, place, row, h, following))
        for other in range(1, rows):
            @pl.when(other > row)
            def _(other=other):
                own_transit(other).wait()
                for h in range(CHUNKS):
                    forward(transit_copy(0, other, h, row))
                    transit_copy(1, other, h, row).start()
        for h in range(CHUNKS):
            spread(row, h)

    lax.fori_loop(col, cols, start_edge, 0)
    late = jnp.where(group == 0, 0, base + TW)
    lax.fori_loop(0, late, start_body, 0)

    @pl.when(group > 0)
    def _():
        for h in range(CHUNKS):
            slab_copy(0, place, row, h, following).wait_recv()
            forward(slab_copy(0, place, row, h, following))
            spread(row, h)
        for other in range(1, rows):
            @pl.when(other > row)
            def _(other=other):
                for h in range(CHUNKS):
                    transit_copy(0, other, h, row).wait_recv()
                    forward(transit_copy(0, other, h, row))
                    transit_copy(1, other, h, row).start()

    lax.fori_loop(late, cols, start_body, 0)

    def spread_again(k):
        for h in range(CHUNKS):
            slab_copy(1, across_place, k, h, across).wait_recv()
            slab_copy(3, across_place, k, h, near).start()

    @pl.when(row < rows - 1)
    def _():
        spread_again(row)

    for copy in own_copies():
        copy.wait()

    moment = row * cols + col
    earliest = memory_ref[col]
    lane = lax.broadcasted_iota(jnp.int32, (orbits, wide), 1)
    half = (lane >= orbits).astype(jnp.int32)
    depth = lax.broadcasted_iota(jnp.int32, (wide, wide), 0)
    depth_half = (depth >= orbits).astype(jnp.int32)

    def energy(direct, mirrored, seen):
        tile = jnp.where(seen, direct.reshape(wide, wide).astype(jnp.float32), 0.0)
        turned = jnp.concatenate(
            [
                jnp.concatenate([tile[:orbits, :orbits], tile[orbits:, :orbits]], axis=1),
                jnp.concatenate([tile[:orbits, orbits:], tile[orbits:, orbits:]], axis=1),
            ],
            axis=0,
        )
        swapped = jnp.dot(
            swap, turned.astype(jnp.bfloat16), preferred_element_type=jnp.float32
        ).astype(jnp.bfloat16)
        swapped = jnp.dot(swapped, swap_t, preferred_element_type=jnp.float32)
        back = mirrored.reshape(wide, wide).astype(jnp.float32).T
        ar, ai = turned[:orbits], turned[orbits:]
        br, bi = swapped[:orbits], swapped[orbits:]
        mr, mi = back[:orbits], back[orbits:]
        fr = ar * br - ai * bi
        fi = ar * bi + ai * br
        return (weight * (fr * mr - fi * mi), weight * (fr * mi + fi * mr))

    def wait_direct(holder, k):
        @pl.when((holder != col) & ((k < row) | (holder <= col)))
        def _():
            for f in range(2):
                direct_copy(f, holder, holder, k).wait_recv()

    for j in range(rows):
        @pl.when(j <= row)
        def _(j=j):
            k = row - j
            if j > 0:
                for h in range(CHUNKS):
                    transit_copy(1, row, h, k).wait_recv()
                    spread(k, h)
                for f in range(2):
                    mirror_copy(f, row, k).wait_recv()
                spread_again(k)

            def one_pair(pair, carry):
                wait_direct(2 * pair, k)
                wait_direct(2 * pair + 1, k)
                at = pl.ds(2 * pair, 2)
                start = k * cols + 2 * pair
                seen = start + depth_half <= moment
                up = energy(direct_greater[at, k], mirror_lesser[k, at], seen)
                down = energy(direct_lesser[at, k], mirror_greater[k, at], seen)
                second = start + half
                live = (second >= earliest) & (second <= moment)
                kept[k, pair] = jnp.concatenate(
                    [
                        jnp.where(live, up[0] - down[0], 0.0),
                        jnp.where(live, up[1] - down[1], 0.0),
                    ],
                    axis=0,
                ).astype(jnp.bfloat16)
                return carry

            lax.fori_loop(0, jnp.where(k < row, cols // 2, col // 2 + 1), one_pair, 0)
            if j == 0:
                @pl.when(row == rows - 1)
                def _():
                    spread_again(row)

    for j in range(rows):
        @pl.when(j <= row)
        def _(j=j):
            k = row - j
            for h in range(CHUNKS):
                slab_copy(2, near_place, k, h, near).wait_recv()
                slab_copy(3, corner_place, k, h, near).wait_recv()

            def one_product(pair, carry):
                at = pl.ds(2 * pair, 2)
                for w in range(TW):
                    total[w] += jnp.dot(
                        kept[k, pair],
                        slab[w, k, at].reshape(wide, wide),
                        preferred_element_type=jnp.float32,
                    )
                return carry

            lax.fori_loop(0, jnp.where(k < row, cols // 2, col // 2 + 1), one_product, 0)

    for w in range(TW):
        whole = total[w]
        out_ref[w, 0] = (
            (whole[:orbits, :orbits] - whole[orbits:, orbits:]) * scaling
        ).astype(jnp.bfloat16)
        out_ref[w, 1] = (
            (whole[:orbits, orbits:] + whole[orbits:, :orbits]) * scaling
        ).astype(jnp.bfloat16)

    def drain_edge(target, carry):
        send_edge(target, lambda copy: copy.wait_send())
        return carry

    def drain_body(target, carry):
        send_body(target, lambda copy: copy.wait_send())
        return carry

    lax.fori_loop(col, cols, drain_edge, 0)
    lax.fori_loop(0, cols, drain_body, 0)
    for h in range(CHUNKS):
        @pl.when(group < groups - 1)
        def _(h=h):
            slab_copy(0, place, row, h, following).wait_send()

    for k in range(rows):
        @pl.when(k <= row)
        def _(k=k):
            for h in range(CHUNKS):
                slab_copy(1, place, k, h, across).wait_send()
                slab_copy(2, place, k, h, near).wait_send()
                slab_copy(3, across_place, k, h, near).wait_send()

    for other in range(1, rows):
        @pl.when(other > row)
        def _(other=other):
            for h in range(CHUNKS):
                @pl.when(group < groups - 1)
                def _(h=h):
                    transit_copy(0, other, h, row).wait_send()

                transit_copy(1, other, h, row).wait_send()

    for other in range(1, rows):
        @pl.when(other > row)
        def _(other=other):
            for f in range(2):
                mirror_copy(f, other, row).wait_send()


def matrices(tiles, orbits):
    first, second, components, _ = tiles.shape
    return (
        tiles.reshape(first, second, components, orbits, orbits)
        .transpose(0, 1, 3, 2, 4)
        .reshape(first, second, orbits, components * orbits)
    )


def per_device(g_greater, g_lesser, coupling, partner, memory_start):
    tile_rows, tile_cols, components, pair_count = g_greater.shape
    rows = lax.axis_size("row")
    cols = lax.axis_size("col")
    orbits = coupling.shape[0]
    wide = 2 * orbits
    scaling = 1.0 / (4.0 * math.sqrt(orbits * tile_rows * rows))
    tile = (orbits, wide)
    vmem = pl.BlockSpec(memory_space=pltpu.VMEM)
    out = pl.pallas_call(
        functools.partial(kernel, rows, cols, scaling),
        out_shape=jax.ShapeDtypeStruct((TW, 2, orbits, orbits), jnp.bfloat16),
        in_specs=[
            pl.BlockSpec(memory_space=pltpu.SMEM),
            pl.BlockSpec(memory_space=pl.ANY),
            pl.BlockSpec(memory_space=pl.ANY),
            vmem,
            vmem,
        ],
        out_specs=vmem,
        scratch_shapes=[
            pltpu.VMEM((cols, rows) + tile, jnp.bfloat16),
            pltpu.VMEM((cols, rows) + tile, jnp.bfloat16),
            pltpu.VMEM((rows, cols) + tile, jnp.bfloat16),
            pltpu.VMEM((rows, cols) + tile, jnp.bfloat16),
            pltpu.VMEM((TW, rows, cols) + tile, jnp.bfloat16),
            pltpu.VMEM((rows, cols) + tile, jnp.bfloat16),
            pltpu.VMEM((rows, cols // 2, wide, wide), jnp.bfloat16),
            pltpu.VMEM((TW, wide, wide), jnp.float32),
            pltpu.SemaphoreType.DMA((2, cols, rows)),
            pltpu.SemaphoreType.DMA((2, cols, rows)),
            pltpu.SemaphoreType.DMA((2, rows)),
            pltpu.SemaphoreType.DMA((2, rows)),
            pltpu.SemaphoreType.DMA((4, rows, CHUNKS)),
            pltpu.SemaphoreType.DMA((TW, rows, CHUNKS)),
            pltpu.SemaphoreType.DMA((2, rows, CHUNKS)),
            pltpu.SemaphoreType.DMA((rows, CHUNKS)),
            pltpu.SemaphoreType.DMA((4 + rows,)),
        ],
        compiler_params=pltpu.CompilerParams(
            collective_id=0, has_side_effects=True, vmem_limit_bytes=48 * 1024 * 1024
        ),
    )(
        memory_start,
        matrices(g_greater, orbits),
        matrices(g_lesser, orbits),
        partner.reshape(1, orbits),
        coupling,
    )
    return out.reshape(1, TW, 2, pair_count)


def solution(mesh):
    return jax.shard_map(
        per_device,
        mesh=mesh,
        in_specs=(P("row", "col", None, None), P("row", "col", None, None), P(), P(), P("row")),
        out_specs=P(("row", "col"), None, None, None),
        check_vma=False,
    )
```

```python
import functools
import math

import jax
import jax.numpy as jnp
from jax import lax
from jax.experimental import pallas as pl
from jax.experimental.pallas import tpu as pltpu
from jax.sharding import PartitionSpec as P

TW = 4
CHUNKS = 8
MESH = pl.DeviceIdType.MESH


def kernel(
    rows,
    cols,
    scaling,
    memory_ref,
    greater_ref,
    lesser_ref,
    partner_ref,
    coupling_ref,
    out_ref,
    direct_greater,
    direct_lesser,
    mirror_greater,
    mirror_lesser,
    slab,
    transit,
    kept,
    total,
    direct_send,
    direct_recv,
    mirror_send,
    mirror_recv,
    slab_send,
    slab_recv,
    transit_send,
    transit_recv,
    own_sem,
):
    row = lax.axis_index("row")
    col = lax.axis_index("col")
    orbits = greater_ref.shape[2]
    wide = 2 * orbits
    groups = cols // TW
    group = col // TW
    place = lax.rem(col, TW)
    base = group * TW
    chunk = cols // CHUNKS
    sources = (greater_ref, lesser_ref)
    directs = (direct_greater, direct_lesser)
    mirrors = (mirror_greater, mirror_lesser)

    barrier = pltpu.get_barrier_semaphore()

    def greet_col(step, carry):
        pl.semaphore_signal(
            barrier, inc=1, device_id=(row, lax.rem(col + step, cols)), device_id_type=MESH
        )
        return carry

    def greet_row(step, carry):
        pl.semaphore_signal(
            barrier, inc=1, device_id=(lax.rem(row + step, rows), col), device_id_type=MESH
        )
        return carry

    lax.fori_loop(1, cols, greet_col, 0)
    lax.fori_loop(1, rows, greet_row, 0)

    def own_copies():
        copies = []
        for f in range(2):
            copies.append(
                pltpu.make_async_copy(sources[f].at[col], directs[f].at[col], own_sem.at[f])
            )
            copies.append(
                pltpu.make_async_copy(
                    sources[f].at[:, row], mirrors[f].at[row], own_sem.at[2 + f]
                )
            )
        return copies

    def own_slab():
        return pltpu.make_async_copy(
            lesser_ref.at[:, row], slab.at[place, row], own_sem.at[4]
        )

    for copy in own_copies():
        copy.start()

    def own_transit(other):
        return pltpu.make_async_copy(
            lesser_ref.at[:, other], transit.at[other], own_sem.at[4 + other]
        )

    @pl.when(group == 0)
    def _():
        own_slab().start()
        for other in range(1, rows):
            @pl.when(other > row)
            def _(other=other):
                own_transit(other).start()

    partners = partner_ref[...]
    partners = jnp.concatenate([partners, partners + orbits], axis=1)
    places = lax.broadcasted_iota(jnp.int32, (wide, wide), 0)
    swap_wide = jnp.where(places == partners, 1.0, 0.0)
    swap_t = swap_wide.astype(jnp.bfloat16)
    swap = swap_wide.T.astype(jnp.bfloat16)
    weight = jnp.concatenate([coupling_ref[...], coupling_ref[...]], axis=1)
    total[...] = jnp.zeros_like(total)

    pl.semaphore_wait(barrier, cols - 1 + rows - 1)

    def mirror_copy(f, other, holder):
        return pltpu.make_async_remote_copy(
            src_ref=sources[f].at[:, other],
            dst_ref=mirrors[f].at[holder],
            send_sem=mirror_send.at[f, other],
            recv_sem=mirror_recv.at[f, holder],
            device_id=(other, col),
            device_id_type=MESH,
        )

    for f in (1, 0):
        for other in range(1, rows):
            @pl.when(other > row)
            def _(other=other, f=f):
                mirror_copy(f, other, row).start()

    def direct_copy(f, target, holder, k):
        return pltpu.make_async_remote_copy(
            src_ref=sources[f].at[target, k],
            dst_ref=directs[f].at[holder, k],
            send_sem=direct_send.at[f, target, k],
            recv_sem=direct_recv.at[f, holder, k],
            device_id=(row, target),
            device_id_type=MESH,
        )

    def send_edge(target, act):
        @pl.when(target != col)
        def _():
            for f in range(2):
                act(direct_copy(f, target, col, row))

    def send_body(target, act):
        @pl.when(target != col)
        def _():
            for k in range(rows - 1):
                @pl.when(k < row)
                def _(k=k):
                    for f in range(2):
                        act(direct_copy(f, target, col, k))

    def start_edge(target, carry):
        send_edge(target, lambda copy: copy.start())
        return carry

    def start_body(target, carry):
        send_body(target, lambda copy: copy.start())
        return carry

    def slab_copy(kind, w, k, h, target):
        return pltpu.make_async_remote_copy(
            src_ref=slab.at[w, k, pl.ds(h * chunk, chunk)],
            dst_ref=slab.at[w, k, pl.ds(h * chunk, chunk)],
            send_sem=slab_send.at[kind, k, h],
            recv_sem=slab_recv.at[w, k, h],
            device_id=(row, target),
            device_id_type=MESH,
        )

    near_place = place + 1 - 2 * lax.rem(place, 2)
    across_place = lax.rem(place + 2, TW)
    corner_place = across_place + 1 - 2 * lax.rem(across_place, 2)
    near = base + near_place
    across = base + across_place
    following = lax.rem(col + TW, cols)

    def transit_copy(kind, other, h, to):
        piece = pl.ds(h * chunk, chunk)
        if kind == 0:
            return pltpu.make_async_remote_copy(
                src_ref=transit.at[other, piece],
                dst_ref=transit.at[other, piece],
                send_sem=transit_send.at[0, other, h],
                recv_sem=transit_recv.at[other, h],
                device_id=(row, following),
                device_id_type=MESH,
            )
        return pltpu.make_async_remote_copy(
            src_ref=transit.at[other, piece],
            dst_ref=slab.at[place, to, piece],
            send_sem=transit_send.at[1, other, h],
            recv_sem=slab_recv.at[place, to, h],
            device_id=(other, col),
            device_id_type=MESH,
        )

    def spread(k, h):
        slab_copy(2, place, k, h, near).start()
        slab_copy(1, place, k, h, across).start()

    def forward(copy):
        @pl.when(group < groups - 1)
        def _():
            copy.start()

    @pl.when(group == 0)
    def _():
        own_slab().wait()
        for h in range(CHUNKS):
            forward(slab_copy(0, place, row, h, following))
        for other in range(1, rows):
            @pl.when(other > row)
            def _(other=other):
                own_transit(other).wait()
                for h in range(CHUNKS):
                    forward(transit_copy(0, other, h, row))
                    transit_copy(1, other, h, row).start()
        for h in range(CHUNKS):
            spread(row, h)

    lax.fori_loop(col, cols, start_edge, 0)
    late = jnp.where(group == 0, 0, base + TW)
    lax.fori_loop(0, late, start_body, 0)

    @pl.when(group > 0)
    def _():
        for h in range(CHUNKS):
            slab_copy(0, place, row, h, following).wait_recv()
            forward(slab_copy(0, place, row, h, following))
            spread(row, h)
        for other in range(1, rows):
            @pl.when(other > row)
            def _(other=other):
                for h in range(CHUNKS):
                    transit_copy(0, other, h, row).wait_recv()
                    forward(transit_copy(0, other, h, row))
                    transit_copy(1, other, h, row).start()

    lax.fori_loop(late, cols, start_body, 0)

    def spread_again(k):
        for h in range(CHUNKS):
            slab_copy(1, across_place, k, h, across).wait_recv()
            slab_copy(3, across_place, k, h, near).start()

    @pl.when(row < rows - 1)
    def _():
        spread_again(row)

    for copy in own_copies():
        copy.wait()

    moment = row * cols + col
    earliest = memory_ref[col]
    lane = lax.broadcasted_iota(jnp.int32, (orbits, wide), 1)
    half = (lane >= orbits).astype(jnp.int32)
    depth = lax.broadcasted_iota(jnp.int32, (wide, wide), 0)
    depth_half = (depth >= orbits).astype(jnp.int32)

    def energy(direct, mirrored, seen):
        tile = jnp.where(seen, direct.reshape(wide, wide).astype(jnp.float32), 0.0)
        turned = jnp.concatenate(
            [
                jnp.concatenate([tile[:orbits, :orbits], tile[orbits:, :orbits]], axis=1),
                jnp.concatenate([tile[:orbits, orbits:], tile[orbits:, orbits:]], axis=1),
            ],
            axis=0,
        )
        swapped = jnp.dot(
            swap, turned.astype(jnp.bfloat16), preferred_element_type=jnp.float32
        ).astype(jnp.bfloat16)
        swapped = jnp.dot(swapped, swap_t, preferred_element_type=jnp.float32)
        back = mirrored.reshape(wide, wide).T.astype(jnp.float32)
        ar, ai = turned[:orbits], turned[orbits:]
        br, bi = swapped[:orbits], swapped[orbits:]
        mr, mi = back[:orbits], back[orbits:]
        fr = ar * br - ai * bi
        fi = ar * bi + ai * br
        return (weight * (fr * mr - fi * mi), weight * (fr * mi + fi * mr))

    def wait_direct(holder, k):
        @pl.when((holder != col) & ((k < row) | (holder <= col)))
        def _():
            for f in range(2):
                direct_copy(f, holder, holder, k).wait_recv()

    def products(k):
        for h in range(CHUNKS):
            slab_copy(2, near_place, k, h, near).wait_recv()
            slab_copy(3, corner_place, k, h, near).wait_recv()

        def one_product(pair, carry):
            at = pl.ds(2 * pair, 2)
            for w in range(TW):
                total[w] += jnp.dot(
                    kept[k, pair],
                    slab[w, k, at].reshape(wide, wide),
                    preferred_element_type=jnp.float32,
                )
            return carry

        lax.fori_loop(0, jnp.where(k < row, cols // 2, col // 2 + 1), one_product, 0)

    for j in range(rows):
        @pl.when(j <= row)
        def _(j=j):
            k = row - j
            if j > 0:
                for h in range(CHUNKS):
                    transit_copy(1, row, h, k).wait_recv()
                    spread(k, h)
                for f in range(2):
                    mirror_copy(f, row, k).wait_recv()
                spread_again(k)
                if j == 1:
                    products(row)

            def one_pair(pair, carry):
                wait_direct(2 * pair, k)
                wait_direct(2 * pair + 1, k)
                at = pl.ds(2 * pair, 2)
                start = k * cols + 2 * pair
                seen = start + depth_half <= moment
                up = energy(direct_greater[at, k], mirror_lesser[k, at], seen)
                down = energy(direct_lesser[at, k], mirror_greater[k, at], seen)
                second = start + half
                live = (second >= earliest) & (second <= moment)
                kept[k, pair] = jnp.concatenate(
                    [
                        jnp.where(live, up[0] - down[0], 0.0),
                        jnp.where(live, up[1] - down[1], 0.0),
                    ],
                    axis=0,
                ).astype(jnp.bfloat16)
                return carry

            lax.fori_loop(0, jnp.where(k < row, cols // 2, col // 2 + 1), one_pair, 0)
            if j == 0:
                @pl.when(row == rows - 1)
                def _():
                    spread_again(row)

    for j in range(rows):
        @pl.when((j <= row) & ((j > 0) | (row == 0)))
        def _(j=j):
            products(row - j)

    for w in range(TW):
        whole = total[w]
        out_ref[w, 0] = (
            (whole[:orbits, :orbits] - whole[orbits:, orbits:]) * scaling
        ).astype(jnp.bfloat16)
        out_ref[w, 1] = (
            (whole[:orbits, orbits:] + whole[orbits:, :orbits]) * scaling
        ).astype(jnp.bfloat16)

    def drain_edge(target, carry):
        send_edge(target, lambda copy: copy.wait_send())
        return carry

    def drain_body(target, carry):
        send_body(target, lambda copy: copy.wait_send())
        return carry

    lax.fori_loop(col, cols, drain_edge, 0)
    lax.fori_loop(0, cols, drain_body, 0)
    for h in range(CHUNKS):
        @pl.when(group < groups - 1)
        def _(h=h):
            slab_copy(0, place, row, h, following).wait_send()

    for k in range(rows):
        @pl.when(k <= row)
        def _(k=k):
            for h in range(CHUNKS):
                slab_copy(1, place, k, h, across).wait_send()
                slab_copy(2, place, k, h, near).wait_send()
                slab_copy(3, across_place, k, h, near).wait_send()

    for other in range(1, rows):
        @pl.when(other > row)
        def _(other=other):
            for h in range(CHUNKS):
                @pl.when(group < groups - 1)
                def _(h=h):
                    transit_copy(0, other, h, row).wait_send()

                transit_copy(1, other, h, row).wait_send()

    for other in range(1, rows):
        @pl.when(other > row)
        def _(other=other):
            for f in range(2):
                mirror_copy(f, other, row).wait_send()


def matrices(tiles, orbits):
    first, second, components, _ = tiles.shape
    return (
        tiles.reshape(first, second, components, orbits, orbits)
        .transpose(0, 1, 3, 2, 4)
        .reshape(first, second, orbits, components * orbits)
    )


def per_device(g_greater, g_lesser, coupling, partner, memory_start):
    tile_rows, tile_cols, components, pair_count = g_greater.shape
    rows = lax.axis_size("row")
    cols = lax.axis_size("col")
    orbits = coupling.shape[0]
    wide = 2 * orbits
    scaling = 1.0 / (4.0 * math.sqrt(orbits * tile_rows * rows))
    tile = (orbits, wide)
    vmem = pl.BlockSpec(memory_space=pltpu.VMEM)
    out = pl.pallas_call(
        functools.partial(kernel, rows, cols, scaling),
        out_shape=jax.ShapeDtypeStruct((TW, 2, orbits, orbits), jnp.bfloat16),
        in_specs=[
            pl.BlockSpec(memory_space=pltpu.SMEM),
            pl.BlockSpec(memory_space=pl.ANY),
            pl.BlockSpec(memory_space=pl.ANY),
            vmem,
            vmem,
        ],
        out_specs=vmem,
        scratch_shapes=[
            pltpu.VMEM((cols, rows) + tile, jnp.bfloat16),
            pltpu.VMEM((cols, rows) + tile, jnp.bfloat16),
            pltpu.VMEM((rows, cols) + tile, jnp.bfloat16),
            pltpu.VMEM((rows, cols) + tile, jnp.bfloat16),
            pltpu.VMEM((TW, rows, cols) + tile, jnp.bfloat16),
            pltpu.VMEM((rows, cols) + tile, jnp.bfloat16),
            pltpu.VMEM((rows, cols // 2, wide, wide), jnp.bfloat16),
            pltpu.VMEM((TW, wide, wide), jnp.float32),
            pltpu.SemaphoreType.DMA((2, cols, rows)),
            pltpu.SemaphoreType.DMA((2, cols, rows)),
            pltpu.SemaphoreType.DMA((2, rows)),
            pltpu.SemaphoreType.DMA((2, rows)),
            pltpu.SemaphoreType.DMA((4, rows, CHUNKS)),
            pltpu.SemaphoreType.DMA((TW, rows, CHUNKS)),
            pltpu.SemaphoreType.DMA((2, rows, CHUNKS)),
            pltpu.SemaphoreType.DMA((rows, CHUNKS)),
            pltpu.SemaphoreType.DMA((4 + rows,)),
        ],
        compiler_params=pltpu.CompilerParams(
            collective_id=0, has_side_effects=True, vmem_limit_bytes=48 * 1024 * 1024
        ),
    )(
        memory_start,
        matrices(g_greater, orbits),
        matrices(g_lesser, orbits),
        partner.reshape(1, orbits),
        coupling,
    )
    return out.reshape(1, TW, 2, pair_count)


def solution(mesh):
    return jax.shard_map(
        per_device,
        mesh=mesh,
        in_specs=(P("row", "col", None, None), P("row", "col", None, None), P(), P(), P("row")),
        out_specs=P(("row", "col"), None, None, None),
        check_vma=False,
    )
```
